32 devices in a mesh: dom: 16 (over z, y, core), help: 2 (over x).
Axes of the slice: x: 2, y: 2, z: 4, core: 2. Of those that a mesh axis runs over, the one named last changes fastest.
Arguments:
- diag_blocks: float32 [256, 128, 128], P(('dom', 'help')), as said below
- up_blocks: float32 [256, 3, 128, 128], P(('dom', 'help')), as said below
- pattern: int32 [256, 6], P(('dom', 'help')), may hold values from 0 to 1, as said below
- vector_in: float32 [256, 128], P(('dom', 'help')), may hold values from -6 to 6
Outputs:
- factor: bfloat16 [256, 7, 128, 128], P(('dom', 'help'))
- applied: float32 [256, 128], P(('dom', 'help'))
The draws below stay inside these ranges and needn't reach their ends.
Inputs may be any that keep to these rules, and one draw needn't show every extreme that they name: A one marks neighbour k of the block row (order +x, -x, +y, -y, +z, -z) as part of its FSAI pattern; ones only where that neighbour lies inside the grid; every block row has two or more ones. Of the 8 block rows of one device (an aligned run of 8 rows) at most 4 have more than two ones and the others have exactly two; the ones beyond the first two of each row number at most 16 on one device, and some device has exactly that many. Every diagonal block is symmetric; the matrix assembled from diag_blocks and up_blocks and every pattern's submatrix are positive definite. `up_blocks`: together with diag_blocks these blocks form the matrix described there.
All inputs are finite; a program needn't handle non-finite values.
Results may differ from the reference program's by a relative error of at most 0.011.
Values may be sent and summed in bfloat16 or wider, within the bound.
A program may use at most 64 MiB of HBM per device.

```python
import jax
import jax.numpy as jnp
from jax import lax

B = 128
BR_DEV = 8
PLANE = 4
GX = 16
GZ = 4
NB = 256


def drawn_modes(key):
    key_shift = jax.random.fold_in(key, 11)
    key_sign = jax.random.fold_in(key, 13)
    shift_value = jax.random.uniform(key_shift, (NB,), jnp.float32, 0.02, 0.04)
    sign_ints = jax.random.randint(key_sign, (NB, B), 0, 2)
    mode_vectors = (2 * sign_ints - 1).astype(jnp.float32) / jnp.sqrt(B * 1.0)
    return (shift_value, mode_vectors)


def draw_diag_blocks(key, part):
    key_noise = jax.random.fold_in(key, 12)
    shift_value, mode_vectors = drawn_modes(key)
    factor_draw = jax.random.normal(key_noise, (NB, B, B), jnp.float32)
    along_mode = jnp.einsum('ra,rab->rb', mode_vectors, factor_draw, precision=lax.Precision.HIGHEST)
    factor_draw = factor_draw - mode_vectors[:, :, None] * along_mode[:, None, :]
    gram_part = jnp.einsum('rab,rcb->rac', factor_draw, factor_draw, precision=lax.Precision.HIGHEST) / (B * 1.0)
    gram_part = 0.5 * (gram_part + jnp.swapaxes(gram_part, -1, -2))
    eye_block = jnp.eye(B, dtype=jnp.float32)
    return gram_part + shift_value[:, None, None] * eye_block[None]


def draw_up_blocks(key, part):
    key_noise = jax.random.fold_in(key, 21)
    key_parity = jax.random.fold_in(key, 31)
    shift_value, mode_vectors = drawn_modes(key)
    noise_scale = (65536.0 * B) ** (-0.5)
    noise = jnp.clip(jax.random.normal(key_noise, (NB, 3, B, B), jnp.float32), -6.0, 6.0)
    noise = noise * noise_scale
    row_ids = jnp.arange(NB, dtype=jnp.int32)
    coord_x = row_ids % GX
    line_parity = jax.random.randint(key_parity, (NB // GX,), 0, 2)
    paired = (coord_x % 2 == line_parity[row_ids // GX]) & (coord_x < GX - 1)
    next_shift = jnp.roll(shift_value, -1, 0)
    next_mode = jnp.roll(mode_vectors, -1, 0)
    strength = jnp.where(paired, 0.8 * jnp.sqrt(shift_value * next_shift), 0.0)
    planted = strength[:, None, None] * mode_vectors[:, :, None] * next_mode[:, None, :]
    return noise.at[:, 0].add(planted)


def draw_pattern(key, part):
    row_ids = jnp.arange(NB, dtype=jnp.int32)
    coord_x = row_ids % GX
    coord_y = row_ids // GX % PLANE
    coord_z = row_ids // (GX * PLANE)
    validity = jnp.stack([coord_x < GX - 1, coord_x > 0, coord_y < PLANE - 1, coord_y > 0, coord_z < GZ - 1, coord_z > 0], 1).astype(jnp.int32)
    device_total = NB // BR_DEV
    line_devices = GX // BR_DEV
    device_ids = jnp.arange(device_total, dtype=jnp.int32)
    heavy_device = jax.random.randint(jax.random.fold_in(key, 3), (device_total,), 0, 3) == 0
    pick_z = jax.random.randint(jax.random.fold_in(key, 7), (), 1, GZ - 1)
    pick_y = jax.random.randint(jax.random.fold_in(key, 8), (), 1, PLANE - 1)
    pick_h = jax.random.randint(jax.random.fold_in(key, 9), (), 0, line_devices)
    forced = (pick_z * PLANE + pick_y) * line_devices + pick_h
    heavy_device = heavy_device | (device_ids == forced)
    inner_x = ((coord_x > 0) & (coord_x < GX - 1)).astype(jnp.int32)
    row_priority = jax.random.randint(jax.random.fold_in(key, 4), (NB,), 0, 1 << 20)
    row_scores = inner_x * (1 << 27) + row_priority * 64 + row_ids % BR_DEV
    row_scores = row_scores.reshape(device_total, BR_DEV)
    row_order = jnp.argsort(-row_scores, axis=1)
    row_ranks = jnp.argsort(row_order, axis=1).reshape(NB)
    heavy_row = heavy_device[row_ids // BR_DEV] & (row_ranks < BR_DEV // 2)
    valid_count = jnp.sum(validity, 1)
    wanted = jnp.where(heavy_row, jnp.minimum(valid_count, 6), 2)
    priority = jax.random.randint(jax.random.fold_in(key, 5), (NB, 6), 0, 8)
    scores = validity * 64 + priority * 8 + (7 - jnp.arange(6, dtype=jnp.int32))[None, :]
    ordering = jnp.argsort(-scores, axis=1)
    slot_ranks = jnp.argsort(ordering, axis=1)
    chosen = (slot_ranks < wanted[:, None]) & (validity > 0)
    return chosen.astype(jnp.int32)


def block_levels(rng, shape, split, least, largest):
    factor_of, own = 1.0, jax.random.fold_in(rng, 6)
    for dim, parts in split:
        heights = jnp.exp(jax.random.uniform(jax.random.fold_in(own, dim), (parts,), jnp.float32, least / len(split), largest / len(split)))
        factor_of = factor_of * jnp.repeat(heights, shape[dim] // parts).reshape([-1 if axis == dim else 1 for axis in range(len(shape))])
    return factor_of


def gaussian(own_key, shape, spread, limit, cuts=(), kind=jnp.bfloat16):
    result = jax.random.normal(own_key, shape, jnp.float32) * spread
    if len(cuts) > 0:
        result = block_levels(own_key, shape, cuts, -0.22, 0.18) * result
    return jnp.clip(result, min=-limit, max=limit).astype(kind)


def setup_inputs(seed: int = 0) -> dict:
    key_of = jax.random.split(jax.random.key(seed), 5)
    diag_blocks = draw_diag_blocks(jax.random.fold_in(key_of[4], 71), 0)
    up_blocks = draw_up_blocks(jax.random.fold_in(key_of[4], 71), 0)
    pattern = draw_pattern(jax.random.fold_in(key_of[4], 71), 0)
    vector_in = gaussian(key_of[3], (NB, B), 1.0, 6.0, ((0, 32),), jnp.float32)
    return {"diag_blocks": diag_blocks, "up_blocks": up_blocks, "pattern": pattern, "vector_in": vector_in}


def grid_layout():
    row_ids = jnp.arange(NB, dtype=jnp.int32)
    coord_x = row_ids % GX
    coord_y = row_ids // GX % PLANE
    coord_z = row_ids // (GX * PLANE)
    validity = jnp.stack([coord_x < GX - 1, coord_x > 0, coord_y < PLANE - 1, coord_y > 0, coord_z < GZ - 1, coord_z > 0], 1)
    strides = jnp.array([1, -1, GX, -GX, GX * PLANE, -GX * PLANE], dtype=jnp.int32)
    neighbour = jnp.clip(row_ids[:, None] + strides[None, :], 0, NB - 1).astype(jnp.int32)
    return (validity, neighbour)

def couplings(up_blocks, selected, near_ids):
    own_up = up_blocks[selected]
    pieces = []
    for dim_index in range(3):
        pieces.append(own_up[:, dim_index])
        far_up = up_blocks[near_ids[:, 2 * dim_index + 1], dim_index]
        pieces.append(jnp.swapaxes(far_up, -1, -2))
    return jnp.stack(pieces, 1)

def reference(diag_blocks, up_blocks, pattern, vector_in):
    validity, neighbour = grid_layout()
    group_rows = GX
    group_total = NB // group_rows
    highest = lax.Precision.HIGHEST

    def matvec_group(group_index):
        selected = (group_index * group_rows + jnp.arange(group_rows, dtype=jnp.int32)).astype(jnp.int32)
        near_ids = neighbour[selected]
        coupled = couplings(up_blocks, selected, near_ids)
        far_terms = jnp.einsum('rkab,rkb->rka', coupled, vector_in[near_ids], precision=highest)
        far_terms = jnp.where(validity[selected][:, :, None], far_terms, 0.0)
        own_term = jnp.einsum('rab,rb->ra', diag_blocks[selected], vector_in[selected], precision=highest)
        return own_term + jnp.sum(far_terms, 1)
    product = lax.map(matvec_group, jnp.arange(group_total, dtype=jnp.int32)).reshape(NB, B)
    identity = jnp.eye(B, dtype=diag_blocks.dtype)

    def factor_group(group_index):
        selected = (group_index * group_rows + jnp.arange(group_rows, dtype=jnp.int32)).astype(jnp.int32)
        near_ids = neighbour[selected]
        coupled = couplings(up_blocks, selected, near_ids)
        weights = pattern[selected].astype(diag_blocks.dtype)
        chol_far = jnp.linalg.cholesky(diag_blocks[near_ids])
        solved = jax.scipy.linalg.cho_solve((chol_far, True), jnp.swapaxes(coupled, -1, -2))
        solved = solved * weights[:, :, None, None]
        schur_block = diag_blocks[selected] - jnp.einsum('rkab,rkbc->rac', coupled, solved, precision=highest)
        chol_schur = jnp.linalg.cholesky(schur_block)
        inverse = jax.scipy.linalg.cho_solve((chol_schur, True), jnp.broadcast_to(identity, schur_block.shape))
        inverse = 0.5 * (inverse + jnp.swapaxes(inverse, -1, -2))
        upper_tri = jnp.swapaxes(jnp.linalg.cholesky(inverse), -1, -2)
        off_blocks = -jnp.einsum('rab,rkcb->rkac', upper_tri, solved, precision=highest)
        row_factor = jnp.concatenate([upper_tri[:, None], off_blocks], 1).astype(jnp.bfloat16)
        widened = row_factor.astype(jnp.float32)
        applied = jnp.einsum('rab,rb->ra', widened[:, 0], product[selected], precision=highest)
        applied = applied + jnp.einsum('rkab,rkb->ra', widened[:, 1:], product[near_ids], precision=highest)
        return (row_factor, applied)
    factor, applied = lax.map(factor_group, jnp.arange(group_total, dtype=jnp.int32))
    return (factor.reshape(NB, 7, B, B), applied.reshape(NB, B))
```

```python
import jax
import jax.numpy as jnp
from jax import lax
from jax.experimental import pallas as pl
from jax.experimental.pallas import tpu as pltpu
from jax.sharding import PartitionSpec as P

PLANE = 4
SUB = 32
HIGH = lax.Precision.HIGHEST
F32 = jnp.float32
BF16 = jnp.bfloat16


def mm(a, b, ca, cb):
    return lax.dot_general(
        a, b, (((ca,), (cb,)), ((), ())), precision=HIGH, preferred_element_type=F32
    )


def mm1(a, b, ca, cb):
    return lax.dot_general(
        a.astype(BF16), b.astype(BF16), (((ca,), (cb,)), ((), ())), preferred_element_type=F32
    )


def small_factors(tiles):
    lane = lax.broadcasted_iota(jnp.int32, (8, 128), 1)
    sub = lax.broadcasted_iota(jnp.int32, (8, 128), 0)
    within = lane % SUB
    base = lane - within
    for j in range(SUB - 1, -1, -1):
        top, at = j // 8, j % 8
        here = within == j
        cols = [jnp.take_along_axis(tiles[t], base + j, axis=1) for t in range(top + 1)]
        scale = lax.rsqrt(cols[top][at : at + 1, :])
        row = jnp.where(here[:1], 1.0, tiles[top][at : at + 1, :]) * scale
        final = jnp.where(within[:1] >= j, row, 0.0)
        for t in range(top + 1):
            new = jnp.where(here, 0.0, tiles[t]) - (cols[t] * scale) * row
            if t == top:
                new = jnp.where(sub < at, new, jnp.where(sub == at, final, tiles[t]))
            tiles[t] = new
    return tiles


def ul_factors(work):
    count, width = work.shape[0], work.shape[1]
    pack = width // SUB
    lane = lax.broadcasted_iota(jnp.int32, (SUB, width), 1)
    sub = lax.broadcasted_iota(jnp.int32, (SUB, width), 0)
    owner = lane // SUB
    for j in range(pack - 1, -1, -1):
        lo = SUB * j
        packed = []
        panels = []
        for g in range(count // pack):
            block = jnp.zeros((SUB, width), F32)
            panel = []
            for b in range(pack):
                rows = work[g * pack + b, lo : lo + SUB, :]
                shift = (SUB * (b - j)) % width
                moved = pltpu.roll(rows, shift, 1) if shift else rows
                block = jnp.where(owner == b, moved, block)
                panel.append(jnp.where(owner == j, (lane - lo == sub).astype(F32), rows))
            packed.append([block[8 * t : 8 * t + 8] for t in range(SUB // 8)])
            panels.append(jnp.concatenate(panel, 0))
        for g in range(count // pack):
            small = jnp.concatenate(small_factors(packed[g]), 0)
            spread = jnp.concatenate(
                [jnp.where(owner == b, small, 0.0) for b in range(pack)], 0
            )
            scaled = mm(spread, panels[g], 1, 0)
            for b in range(pack):
                at = g * pack + b
                v = scaled[SUB * b : SUB * b + SUB]
                work[at, lo : lo + SUB, :] = jnp.where(lane >= lo, v, 0.0)
                if lo:
                    change = mm(v, v, 0, 0)
                    full = lax.broadcasted_iota(jnp.int32, (lo, width), 1) // SUB
                    work[at, :lo, :] = jnp.where(full == j, 0.0, work[at, :lo, :]) - change[:lo]


def inverse_kernel(diag_ref, inv_ref, low_ref, work):
    work[...] = diag_ref[...]
    ul_factors(work)

    def body(r, carry):
        y = work[r]
        inv = mm(y, y, 0, 0)
        inv_ref[r] = inv
        low_ref[r] = inv.astype(BF16)
        return carry

    lax.fori_loop(0, work.shape[0], body, 0)


def rows_kernel(
    pattern_ref, diag_ref, up_ref, ux_ref, dx_ref, cy_ref, cz_ref, yu_ref, yl_ref, zu_ref,
    zl_ref, prod_ref, near_ref, factor_ref, applied_ref, work, solved
):
    count = work.shape[0]

    def gather(r, carry):
        schur = diag_ref[r]

        def term(k, inv, coupling, plus, mul):
            w = pattern_ref[r, k].astype(F32) * mul(inv, coupling, 1, 1 if plus else 0)
            solved[r, k] = w
            return mul(coupling, w, 1 if plus else 0, 0)

        schur = schur - term(0, dx_ref[r + 2], ux_ref[r + 1], True, mm)
        schur = schur - term(1, dx_ref[r], ux_ref[r], False, mm)
        schur = schur - term(2, yu_ref[r], up_ref[r, 1], True, mm1)
        schur = schur - term(3, yl_ref[r], cy_ref[r], False, mm1)
        schur = schur - term(4, zu_ref[r], up_ref[r, 2], True, mm1)
        schur = schur - term(5, zl_ref[r], cz_ref[r], False, mm1)
        work[r] = schur
        return carry

    lax.fori_loop(0, count, gather, 0)
    ul_factors(work)

    def finish(r, carry):
        y = work[r]
        low = y.astype(BF16)
        factor_ref[r, 0] = low
        total = mm(prod_ref[...][None][0], low.astype(F32), 1, 1)
        for k in range(6):
            block = (-(mm if k < 2 else mm1)(y, solved[r, k], 1, 1)).astype(BF16)
            factor_ref[r, 1 + k] = block
            total = total + mm(near_ref[k], block.astype(F32), 1, 1)
        keep = lax.broadcasted_iota(jnp.int32, total.shape, 0) == r
        applied_ref[...] = jnp.where(keep, total, applied_ref[...])
        return carry

    applied_ref[...] = jnp.zeros_like(applied_ref)
    lax.fori_loop(0, count, finish, 0)


def passed_along(block, axis, distance):
    devices = range(lax.axis_size(axis))
    route = [(i - distance, i) for i in devices if i - distance in devices]
    return lax.ppermute(block, axis, route)


VM = pl.BlockSpec(memory_space=pltpu.VMEM)
SM = pl.BlockSpec(memory_space=pltpu.SMEM)


def local(diag_blocks, up_blocks, pattern, vector_in):
    rows, width = diag_blocks.shape[0], diag_blocks.shape[1]
    helper = lax.axis_index("help")
    domain = lax.axis_index("dom")
    help_count = lax.axis_size("help")
    dom_count = lax.axis_size("dom")
    inv, low = pl.pallas_call(
        inverse_kernel,
        out_shape=(
            jax.ShapeDtypeStruct((rows, width, width), F32),
            jax.ShapeDtypeStruct((rows, width, width), BF16),
        ),
        in_specs=[VM],
        out_specs=(VM, VM),
        scratch_shapes=[pltpu.VMEM((rows, width, width), F32)],
        name="inverses",
    )(diag_blocks)
    up_x = up_blocks[:, 0]
    c_y = passed_along(up_blocks[:, 1].astype(BF16), "dom", 1)
    c_z = passed_along(up_blocks[:, 2].astype(BF16), "dom", PLANE)
    c_x = passed_along(up_x[-1:], "help", 1)
    own_t = jnp.einsum("rdab,ra->drb", up_blocks, vector_in, precision=HIGH)

    def near_rows(vec, lower_edge, upper_edge, vec_low, axis_low):
        return vec

    def spread(vec):
        up_edge = passed_along(vec[:1], "help", -1)
        low_edge = passed_along(vec[-1:], "help", 1)
        return jnp.stack(
            [
                jnp.concatenate([vec[1:], up_edge], 0),
                jnp.concatenate([low_edge, vec[:-1]], 0),
                passed_along(vec, "dom", -1),
                passed_along(vec, "dom", 1),
                passed_along(vec, "dom", -PLANE),
                passed_along(vec, "dom", PLANE),
            ]
        )

    x_up = jnp.concatenate([vector_in[1:], passed_along(vector_in[:1], "help", -1)], 0)
    y_up = passed_along(vector_in, "dom", -1)
    z_up = passed_along(vector_in, "dom", -PLANE)
    x_low = jnp.concatenate([passed_along(own_t[0, -1:], "help", 1), own_t[0, :-1]], 0)
    y_low = passed_along(own_t[1], "dom", 1)
    z_low = passed_along(own_t[2], "dom", PLANE)
    coord_y = domain % PLANE
    zero = jnp.zeros_like(vector_in)
    uppers = jnp.stack(
        [
            x_up,
            jnp.where(coord_y < PLANE - 1, y_up, zero),
            jnp.where(domain + PLANE < dom_count, z_up, zero),
        ],
        1,
    )
    product = (
        jnp.einsum("rab,rb->ra", diag_blocks, vector_in, precision=HIGH)
        + jnp.einsum("rdab,rdb->ra", up_blocks, uppers, precision=HIGH)
        + x_low
        + jnp.where(coord_y > 0, y_low, zero)
        + jnp.where(domain >= PLANE, z_low, zero)
    )
    near = spread(product)
    d_x = jnp.concatenate(
        [passed_along(inv[-1:], "help", 1), inv, passed_along(inv[:1], "help", -1)], 0
    )
    u_x = jnp.concatenate([c_x, up_x], 0)
    yu = passed_along(low, "dom", -1)
    yl = passed_along(low, "dom", 1)
    zu = passed_along(low, "dom", -PLANE)
    zl = passed_along(low, "dom", PLANE)
    factor, applied = pl.pallas_call(
        rows_kernel,
        out_shape=(
            jax.ShapeDtypeStruct((rows, 7, width, width), BF16),
            jax.ShapeDtypeStruct((rows, width), F32),
        ),
        in_specs=[SM] + [VM] * 12,
        out_specs=(VM, VM),
        scratch_shapes=[
            pltpu.VMEM((rows, width, width), F32),
            pltpu.VMEM((rows, 6, width, width), F32),
        ],
        name="rows",
        compiler_params=pltpu.CompilerParams(vmem_limit_bytes=40 << 20),
    )(pattern, diag_blocks, up_blocks, u_x, d_x, c_y, c_z, yu, yl, zu, zl, product, near)
    return (factor, applied)


def solution(mesh):
    in_specs = (
        P(("dom", "help"), None, None),
        P(("dom", "help"), None, None, None),
        P(("dom", "help"), None),
        P(("dom", "help"), None),
    )
    out_specs = (P(("dom", "help"), None, None, None), P(("dom", "help"), None))
    return jax.shard_map(local, mesh=mesh, in_specs=in_specs, out_specs=out_specs, check_vma=False)
```

```python
import functools

import jax
import jax.numpy as jnp
from jax import lax
from jax.experimental import pallas as pl
from jax.experimental.pallas import tpu as pltpu
from jax.sharding import PartitionSpec as P

PLANE = 4
SUB = 32
MESSAGES = 25
HIGH = lax.Precision.HIGHEST
F32 = jnp.float32
BF16 = jnp.bfloat16


def mm(a, b, ca, cb):
    return lax.dot_general(
        a, b, (((ca,), (cb,)), ((), ())), precision=HIGH, preferred_element_type=F32
    )


def mm1(a, b, ca, cb):
    return lax.dot_general(
        a.astype(BF16), b.astype(BF16), (((ca,), (cb,)), ((), ())), preferred_element_type=F32
    )


def halves(a):
    high = a.astype(BF16)
    return high, (a - high.astype(F32)).astype(BF16)


def mm3(a, b, ca, cb):
    (ah, al), (bh, bl) = halves(a), halves(b)
    return mm1(ah, bh, ca, cb) + (mm1(ah, bl, ca, cb) + mm1(al, bh, ca, cb))


def small_factors(tiles):
    lane = lax.broadcasted_iota(jnp.int32, (8, 128), 1)
    sub = lax.broadcasted_iota(jnp.int32, (8, 128), 0)
    within = lane % SUB
    base = lane - within
    for j in range(SUB - 1, -1, -1):
        top, at = j // 8, j % 8
        here = within == j
        cols = [jnp.take_along_axis(tiles[t], base + j, axis=1) for t in range(top + 1)]
        scale = lax.rsqrt(cols[top][at : at + 1, :])
        row = jnp.where(here[:1], 1.0, tiles[top][at : at + 1, :]) * scale
        final = jnp.where(within[:1] >= j, row, 0.0)
        for t in range(top + 1):
            new = jnp.where(here, 0.0, tiles[t]) - (cols[t] * scale) * row
            if t == top:
                new = jnp.where(sub < at, new, jnp.where(sub == at, final, tiles[t]))
            tiles[t] = new
    return tiles


def ul_factors(work, between=None):
    count, width = work.shape[0], work.shape[1]
    pack = width // SUB
    lane = lax.broadcasted_iota(jnp.int32, (SUB, width), 1)
    sub = lax.broadcasted_iota(jnp.int32, (SUB, width), 0)
    owner = lane // SUB
    for j in range(pack - 1, -1, -1):
        lo = SUB * j
        packed = []
        panels = []
        for g in range(count // pack):
            block = jnp.zeros((SUB, width), F32)
            panel = []
            for b in range(pack):
                rows = work[g * pack + b, lo : lo + SUB, :]
                shift = (SUB * (b - j)) % width
                moved = pltpu.roll(rows, shift, 1) if shift else rows
                block = jnp.where(owner == b, moved, block)
                panel.append(jnp.where(owner == j, (lane - lo == sub).astype(F32), rows))
            packed.append([block[8 * t : 8 * t + 8] for t in range(SUB // 8)])
            panels.append(jnp.concatenate(panel, 0))
        for g in range(count // pack):
            small = jnp.concatenate(small_factors(packed[g]), 0)
            spread = jnp.concatenate(
                [jnp.where(owner == b, small, 0.0) for b in range(pack)], 0
            )
            scaled = mm(spread, panels[g], 1, 0)
            for b in range(pack):
                at = g * pack + b
                v = scaled[SUB * b : SUB * b + SUB]
                work[at, lo : lo + SUB, :] = jnp.where(lane >= lo, v, 0.0)
                if lo:
                    change = mm(v, v, 0, 0)
                    full = lax.broadcasted_iota(jnp.int32, (lo, width), 1) // SUB
                    work[at, :lo, :] = jnp.where(full == j, 0.0, work[at, :lo, :]) - change[:lo]
        if between:
            between(j)


def exchange_kernel(
    line_count, dom_count, diag_ref, up_ref, x_ref, prod_ref, near_ref, dx_ref, edge_ref, cy_ref,
    cz_ref, yu_ref, yl_ref, zu_ref, zl_ref, work, cy_own, cz_own, low, upt, from_up, from_low,
    prod_up, prod_low, send_sem, recv_sem
):
    rows = x_ref.shape[0]
    dom = lax.axis_index("dom")
    line = lax.axis_index("help")
    spot = lax.rem(dom, PLANE)
    exists = (
        (line < line_count - 1, line > 0),
        (spot < PLANE - 1, spot > 0),
        (dom + PLANE < dom_count, dom >= PLANE),
    )
    target = (
        ((dom, line + 1), (dom, line - 1)),
        ((dom + 1, line), (dom - 1, line)),
        ((dom + PLANE, line), (dom - PLANE, line)),
    )
    barrier = pltpu.get_barrier_semaphore()
    partners = jnp.int32(0)
    for d in range(3):
        for s in range(2):
            partners = partners + exists[d][s].astype(jnp.int32)

            @pl.when(exists[d][s])
            def _(d=d, s=s):
                pl.semaphore_signal(
                    barrier, inc=1, device_id=target[d][s], device_id_type=pl.DeviceIdType.MESH
                )

    pl.semaphore_wait(barrier, partners)
    messages = []

    def send(d, s, src, dst):
        m = len(messages)
        copy = pltpu.make_async_remote_copy(
            src_ref=src,
            dst_ref=dst,
            send_sem=send_sem.at[m],
            recv_sem=recv_sem.at[m],
            device_id=target[d][s],
            device_id_type=pl.DeviceIdType.MESH,
        )
        messages.append((d, s, copy))

        @pl.when(exists[d][s])
        def _():
            copy.start()

        return m

    def received(ids):
        for m in ids:
            d, s, copy = messages[m]

            @pl.when(exists[d][1 - s])
            def _(copy=copy):
                copy.wait_recv()

    def blank(d, s, ref):
        @pl.when(jnp.logical_not(exists[d][s]))
        def _():
            ref[...] = jnp.zeros_like(ref)

    blank(0, 1, edge_ref)
    blank(1, 1, cy_ref)
    blank(2, 1, cz_ref)
    blank(0, 1, dx_ref.at[0])
    blank(0, 0, dx_ref.at[rows + 1])
    blank(1, 0, yu_ref)
    blank(1, 1, yl_ref)
    blank(2, 0, zu_ref)
    blank(2, 1, zl_ref)
    for d in range(3):
        blank(d, 0, from_up.at[d])
        blank(d, 1, from_low.at[d])
        blank(d, 0, prod_up.at[d])
        blank(d, 1, prod_low.at[d])
    first = [send(d, 1, x_ref, from_up.at[d]) for d in range(3)]
    late = [send(0, 0, up_ref.at[rows - 1, 0], edge_ref.at[0])]
    cy_own[...] = up_ref[:, 1].astype(BF16)
    cz_own[...] = up_ref[:, 2].astype(BF16)
    vec = x_ref[...]
    at_row = lax.broadcasted_iota(jnp.int32, vec.shape, 0)
    for d in range(3):
        total = jnp.zeros_like(vec)
        for r in range(rows):
            total = jnp.where(at_row == r, mm(vec, up_ref[r, d], 1, 0), total)
        upt[d] = total
    for d in range(3):
        first.append(send(d, 0, upt.at[d], from_low.at[d]))
    late.append(send(1, 0, cy_own, cy_ref))
    late.append(send(2, 0, cz_own, cz_ref))
    work[...] = diag_ref[...]

    def above(own, edge):
        return jnp.where(at_row == rows - 1, edge[:1], pltpu.roll(own, rows - 1, 0))

    def below(own, edge):
        return jnp.where(at_row == 0, edge[rows - 1 : rows], pltpu.roll(own, 1, 0))

    def between(j):
        if j == work.shape[1] // SUB - 1:
            received(first)
            total = below(upt[0], from_low[0]) + from_low[1] + from_low[2]
            ups = [above(vec, from_up[0]), from_up[1], from_up[2]]
            for r in range(rows):
                part = mm(vec, diag_ref[r], 1, 1)
                for d in range(3):
                    part = part + mm(ups[d], up_ref[r, d], 1, 1)
                total = total + jnp.where(at_row == r, part, 0.0)
            prod_ref[...] = total
        if j == work.shape[1] // SUB - 2:
            for d in range(3):
                late.append(send(d, 1, prod_ref, prod_up.at[d]))
                late.append(send(d, 0, prod_ref, prod_low.at[d]))

    ul_factors(work, between)
    half = rows // 2
    for h in range(2):
        for r in range(half * h, half * h + half):
            y = work[r]
            inv = mm(y, y, 0, 0)
            dx_ref[r + 1] = inv
            low[r] = inv.astype(BF16)
        part = pl.ds(half * h, half)
        late.append(send(2, 0, low.at[part], zl_ref.at[part]))
        late.append(send(2, 1, low.at[part], zu_ref.at[part]))
        late.append(send(1, 0, low.at[part], yl_ref.at[part]))
        late.append(send(1, 1, low.at[part], yu_ref.at[part]))
        if h:
            late.append(send(0, 0, dx_ref.at[rows], dx_ref.at[0]))
        else:
            late.append(send(0, 1, dx_ref.at[1], dx_ref.at[rows + 1]))
    received(late)
    total = prod_ref[...]
    near_ref[0] = above(total, prod_up[0])
    near_ref[1] = below(total, prod_low[0])
    near_ref[2] = prod_up[1]
    near_ref[3] = prod_low[1]
    near_ref[4] = prod_up[2]
    near_ref[5] = prod_low[2]
    for d, s, copy in messages:

        @pl.when(exists[d][s])
        def _(copy=copy):
            copy.wait_send()


def rows_kernel(
    pattern_ref, diag_ref, up_ref, edge_ref, dx_ref, cy_ref, cz_ref, yu_ref, yl_ref, zu_ref,
    zl_ref, prod_ref, near_ref, factor_ref, applied_ref, work, solved
):
    count = work.shape[0]

    def gather(r, carry):
        schur = diag_ref[r]

        def term(k, inv, coupling, plus, mul):
            w = pattern_ref[r, k].astype(F32) * mul(inv, coupling, 1, 1 if plus else 0)
            solved[r, k] = w
            return mul(coupling, w, 1 if plus else 0, 0)

        lower = jnp.where(r == 0, edge_ref[0], up_ref[jnp.maximum(r - 1, 0), 0])
        schur = schur - term(0, dx_ref[r + 2], up_ref[r, 0], True, mm3)
        schur = schur - term(1, dx_ref[r], lower, False, mm3)
        schur = schur - term(2, yu_ref[r], up_ref[r, 1], True, mm1)
        schur = schur - term(3, yl_ref[r], cy_ref[r], False, mm1)
        schur = schur - term(4, zu_ref[r], up_ref[r, 2], True, mm1)
        schur = schur - term(5, zl_ref[r], cz_ref[r], False, mm1)
        work[r] = schur
        return carry

    lax.fori_loop(0, count, gather, 0)
    ul_factors(work)

    def split(v):
        high = v.astype(BF16).astype(F32)
        rest = v - high
        mid = rest.astype(BF16).astype(F32)
        return jnp.concatenate([high, mid, rest - mid], 0)

    def finish(r, carry):
        y = work[r]
        low = y.astype(BF16)
        factor_ref[r, 0] = low
        total = mm1(split(prod_ref[...]), low, 1, 1)
        for k in range(6):
            block = (-(mm3 if k < 2 else mm1)(y, solved[r, k], 1, 1)).astype(BF16)
            factor_ref[r, 1 + k] = block
            total = total + mm1(split(near_ref[k]), block, 1, 1)
        total = total[:count] + total[count : 2 * count] + total[2 * count :]
        keep = lax.broadcasted_iota(jnp.int32, total.shape, 0) == r
        applied_ref[...] = jnp.where(keep, total, applied_ref[...])
        return carry

    applied_ref[...] = jnp.zeros_like(applied_ref)
    lax.fori_loop(0, count, finish, 0)


VM = pl.BlockSpec(memory_space=pltpu.VMEM)
SM = pl.BlockSpec(memory_space=pltpu.SMEM)


def local(diag_blocks, up_blocks, pattern, vector_in):
    rows, width = diag_blocks.shape[0], diag_blocks.shape[1]
    block = jax.ShapeDtypeStruct((rows, width, width), BF16)
    vec = pltpu.VMEM((3, rows, width), F32)
    stack = pltpu.VMEM((rows, width, width), BF16)
    prod, near, dx, edge, cy, cz, yu, yl, zu, zl = pl.pallas_call(
        functools.partial(exchange_kernel, lax.axis_size("help"), lax.axis_size("dom")),
        out_shape=(
            jax.ShapeDtypeStruct((rows, width), F32),
            jax.ShapeDtypeStruct((6, rows, width), F32),
            jax.ShapeDtypeStruct((rows + 2, width, width), F32),
            jax.ShapeDtypeStruct((1, width, width), F32),
        )
        + (block,) * 6,
        in_specs=[VM] * 3,
        out_specs=(VM,) * 10,
        scratch_shapes=[pltpu.VMEM((rows, width, width), F32)]
        + [stack] * 3
        + [vec] * 5
        + [pltpu.SemaphoreType.DMA((MESSAGES,)), pltpu.SemaphoreType.DMA((MESSAGES,))],
        name="exchange",
        compiler_params=pltpu.CompilerParams(
            collective_id=0, has_side_effects=True, vmem_limit_bytes=40 << 20
        ),
    )(diag_blocks, up_blocks, vector_in)
    factor, applied = pl.pallas_call(
        rows_kernel,
        out_shape=(
            jax.ShapeDtypeStruct((rows, 7, width, width), BF16),
            jax.ShapeDtypeStruct((rows, width), F32),
        ),
        in_specs=[SM] + [VM] * 12,
        out_specs=(VM, VM),
        scratch_shapes=[
            pltpu.VMEM((rows, width, width), F32),
            pltpu.VMEM((rows, 6, width, width), F32),
        ],
        name="rows",
        compiler_params=pltpu.CompilerParams(vmem_limit_bytes=40 << 20),
    )(pattern, diag_blocks, up_blocks, edge, dx, cy, cz, yu, yl, zu, zl, prod, near)
    return (factor, applied)


def solution(mesh):
    in_specs = (
        P(("dom", "help"), None, None),
        P(("dom", "help"), None, None, None),
        P(("dom", "help"), None),
        P(("dom", "help"), None),
    )
    out_specs = (P(("dom", "help"), None, None, None), P(("dom", "help"), None))
    return jax.shard_map(local, mesh=mesh, in_specs=in_specs, out_specs=out_specs, check_vma=False)
```

```python
import functools

import jax
import jax.numpy as jnp
from jax import lax
from jax.experimental import pallas as pl
from jax.experimental.pallas import tpu as pltpu
from jax.sharding import PartitionSpec as P

PLANE = 4
SUB = 32
MESSAGES = 25
HIGH = lax.Precision.HIGHEST
F32 = jnp.float32
BF16 = jnp.bfloat16


def mm(a, b, ca, cb):
    return lax.dot_general(
        a, b, (((ca,), (cb,)), ((), ())), precision=HIGH, preferred_element_type=F32
    )


def mm1(a, b, ca, cb):
    return lax.dot_general(
        a.astype(BF16), b.astype(BF16), (((ca,), (cb,)), ((), ())), preferred_element_type=F32
    )


def halves(a):
    high = a.astype(BF16)
    return high, (a - high.astype(F32)).astype(BF16)


def mm3(a, b, ca, cb):
    (ah, al), (bh, bl) = halves(a), halves(b)
    return mm1(ah, bh, ca, cb) + (mm1(ah, bl, ca, cb) + mm1(al, bh, ca, cb))


def split(v):
    high = v.astype(BF16).astype(F32)
    rest = v - high
    mid = rest.astype(BF16).astype(F32)
    return jnp.concatenate([high, mid, rest - mid], 0).astype(BF16)


def mv(parts, matrix, cb):
    high, low = halves(matrix)
    total = mm1(parts, high, 1, cb) + mm1(parts, low, 1, cb)
    n = total.shape[0] // 3
    return total[:n] + (total[n : 2 * n] + total[2 * n :])


def small_factors(groups):
    lane = lax.broadcasted_iota(jnp.int32, (8, 128), 1)
    sub = lax.broadcasted_iota(jnp.int32, (8, 128), 0)
    within = lane % SUB
    base = lane - within
    for top in range(SUB // 8 - 1, -1, -1):
        ahead = [
            [
                [jnp.take_along_axis(tiles[t], base + 8 * top + i, axis=1) for t in range(top + 1)]
                for i in range(8)
            ]
            for tiles in groups
        ]
        for at in range(7, -1, -1):
            j = 8 * top + at
            here = within == j
            for tiles, cols in zip(groups, ahead):
                scale = lax.rsqrt(cols[at][top][at : at + 1, :])
                scaled = [cols[at][t] * scale for t in range(top + 1)]
                for i in range(at - 1, -1, -1):
                    weight = cols[i][top][at : at + 1, :] * scale
                    cols[i] = [cols[i][t] - scaled[t] * weight for t in range(top + 1)]
                row = jnp.where(here[:1], 1.0, tiles[top][at : at + 1, :]) * scale
                final = jnp.where(within[:1] >= j, row, 0.0)
                for t in range(top + 1):
                    new = jnp.where(here, 0.0, tiles[t]) - scaled[t] * row
                    if t == top:
                        new = jnp.where(sub < at, new, jnp.where(sub == at, final, tiles[t]))
                    tiles[t] = new
    return groups


def ul_factors(work, between=None):
    count, width = work.shape[0], work.shape[1]
    pack = width // SUB
    lane = lax.broadcasted_iota(jnp.int32, (SUB, width), 1)
    sub = lax.broadcasted_iota(jnp.int32, (SUB, width), 0)
    owner = lane // SUB
    for j in range(pack - 1, -1, -1):
        lo = SUB * j
        packed = []
        panels = []
        for g in range(count // pack):
            block = jnp.zeros((SUB, width), F32)
            panel = []
            for b in range(pack):
                rows = work[g * pack + b, lo : lo + SUB, :]
                shift = (SUB * (b - j)) % width
                moved = pltpu.roll(rows, shift, 1) if shift else rows
                block = jnp.where(owner == b, moved, block)
                panel.append(jnp.where(owner == j, (lane - lo == sub).astype(F32), rows))
            packed.append([block[8 * t : 8 * t + 8] for t in range(SUB // 8)])
            panels.append(jnp.concatenate(panel, 0))
        small_factors(packed)
        for g in range(count // pack):
            small = jnp.concatenate(packed[g], 0)
            spread = jnp.concatenate(
                [jnp.where(owner == b, small, 0.0) for b in range(pack)], 0
            )
            scaled = mm3(spread, panels[g], 1, 0)
            for b in range(pack):
                at = g * pack + b
                v = scaled[SUB * b : SUB * b + SUB]
                work[at, lo : lo + SUB, :] = jnp.where(lane >= lo, v, 0.0)
                if lo:
                    change = mm3(v, v, 0, 0)
                    full = lax.broadcasted_iota(jnp.int32, (lo, width), 1) // SUB
                    work[at, :lo, :] = jnp.where(full == j, 0.0, work[at, :lo, :]) - change[:lo]
        if between:
            between(j)


def exchange_kernel(
    line_count, dom_count, diag_ref, up_ref, x_ref, prod_ref, near_ref, dx_ref, edge_ref, cy_ref,
    cz_ref, yu_ref, yl_ref, zu_ref, zl_ref, work, cy_own, cz_own, low, upt, from_up, from_low,
    prod_up, prod_low, send_sem, recv_sem
):
    rows = x_ref.shape[0]
    dom = lax.axis_index("dom")
    line = lax.axis_index("help")
    spot = lax.rem(dom, PLANE)
    exists = (
        (line < line_count - 1, line > 0),
        (spot < PLANE - 1, spot > 0),
        (dom + PLANE < dom_count, dom >= PLANE),
    )
    target = (
        ((dom, line + 1), (dom, line - 1)),
        ((dom + 1, line), (dom - 1, line)),
        ((dom + PLANE, line), (dom - PLANE, line)),
    )
    barrier = pltpu.get_barrier_semaphore()
    partners = jnp.int32(0)
    for d in range(3):
        for s in range(2):
            partners = partners + exists[d][s].astype(jnp.int32)

            @pl.when(exists[d][s])
            def _(d=d, s=s):
                pl.semaphore_signal(
                    barrier, inc=1, device_id=target[d][s], device_id_type=pl.DeviceIdType.MESH
                )

    pl.semaphore_wait(barrier, partners)
    messages = []

    def send(d, s, src, dst):
        m = len(messages)
        copy = pltpu.make_async_remote_copy(
            src_ref=src,
            dst_ref=dst,
            send_sem=send_sem.at[m],
            recv_sem=recv_sem.at[m],
            device_id=target[d][s],
            device_id_type=pl.DeviceIdType.MESH,
        )
        messages.append((d, s, copy))

        @pl.when(exists[d][s])
        def _():
            copy.start()

        return m

    def received(ids):
        for m in ids:
            d, s, copy = messages[m]

            @pl.when(exists[d][1 - s])
            def _(copy=copy):
                copy.wait_recv()

    def blank(d, s, ref):
        @pl.when(jnp.logical_not(exists[d][s]))
        def _():
            ref[...] = jnp.zeros_like(ref)

    blank(0, 1, edge_ref)
    blank(1, 1, cy_ref)
    blank(2, 1, cz_ref)
    blank(0, 1, dx_ref.at[0])
    blank(0, 0, dx_ref.at[rows + 1])
    blank(1, 0, yu_ref)
    blank(1, 1, yl_ref)
    blank(2, 0, zu_ref)
    blank(2, 1, zl_ref)
    for d in range(3):
        blank(d, 0, from_up.at[d])
        blank(d, 1, from_low.at[d])
        blank(d, 0, prod_up.at[d])
        blank(d, 1, prod_low.at[d])
    first = [send(d, 1, x_ref, from_up.at[d]) for d in range(3)]
    late = [send(0, 0, up_ref.at[rows - 1, 0], edge_ref.at[0])]
    cy_own[...] = up_ref[:, 1].astype(BF16)
    cz_own[...] = up_ref[:, 2].astype(BF16)
    vec = x_ref[...]
    parts = split(vec)
    at_row = lax.broadcasted_iota(jnp.int32, vec.shape, 0)
    for d in range(3):
        total = jnp.zeros_like(vec)
        for r in range(rows):
            total = jnp.where(at_row == r, mv(parts, up_ref[r, d], 0), total)
        upt[d] = total
    for d in range(3):
        first.append(send(d, 0, upt.at[d], from_low.at[d]))
    late.append(send(1, 0, cy_own, cy_ref))
    late.append(send(2, 0, cz_own, cz_ref))
    work[...] = diag_ref[...]

    def above(own, edge):
        return jnp.where(at_row == rows - 1, edge[:1], pltpu.roll(own, rows - 1, 0))

    def below(own, edge):
        return jnp.where(at_row == 0, edge[rows - 1 : rows], pltpu.roll(own, 1, 0))

    def between(j):
        if j == work.shape[1] // SUB - 1:
            received(first)
            total = below(upt[0], from_low[0]) + from_low[1] + from_low[2]
            ups = [split(v) for v in (above(vec, from_up[0]), from_up[1], from_up[2])]
            for r in range(rows):
                part = mv(parts, diag_ref[r], 1)
                for d in range(3):
                    part = part + mv(ups[d], up_ref[r, d], 1)
                total = total + jnp.where(at_row == r, part, 0.0)
            prod_ref[...] = total
        if j == work.shape[1] // SUB - 2:
            for d in range(3):
                late.append(send(d, 1, prod_ref, prod_up.at[d]))
                late.append(send(d, 0, prod_ref, prod_low.at[d]))

    ul_factors(work, between)
    half = rows // 2
    for h in range(2):
        for r in range(half * h, half * h + half):
            y = work[r]
            inv = mm3(y, y, 0, 0)
            dx_ref[r + 1] = inv
            low[r] = inv.astype(BF16)
        part = pl.ds(half * h, half)
        late.append(send(2, 0, low.at[part], zl_ref.at[part]))
        late.append(send(2, 1, low.at[part], zu_ref.at[part]))
        late.append(send(1, 0, low.at[part], yl_ref.at[part]))
        late.append(send(1, 1, low.at[part], yu_ref.at[part]))
        if h:
            late.append(send(0, 0, dx_ref.at[rows], dx_ref.at[0]))
        else:
            late.append(send(0, 1, dx_ref.at[1], dx_ref.at[rows + 1]))
    received(late)
    total = prod_ref[...]
    near_ref[0] = above(total, prod_up[0])
    near_ref[1] = below(total, prod_low[0])
    near_ref[2] = prod_up[1]
    near_ref[3] = prod_low[1]
    near_ref[4] = prod_up[2]
    near_ref[5] = prod_low[2]
    for d, s, copy in messages:

        @pl.when(exists[d][s])
        def _(copy=copy):
            copy.wait_send()


def rows_kernel(
    pattern_ref, diag_ref, up_ref, edge_ref, dx_ref, cy_ref, cz_ref, yu_ref, yl_ref, zu_ref,
    zl_ref, prod_ref, near_ref, factor_ref, applied_ref, work, solved
):
    count = work.shape[0]

    def gather(r, carry):
        schur = diag_ref[r]

        def term(k, inv, coupling, plus, mul):
            w = pattern_ref[r, k].astype(F32) * mul(inv, coupling, 1, 1 if plus else 0)
            solved[r, k] = w
            return mul(coupling, w, 1 if plus else 0, 0)

        lower = jnp.where(r == 0, edge_ref[0], up_ref[jnp.maximum(r - 1, 0), 0])
        schur = schur - term(0, dx_ref[r + 2], up_ref[r, 0], True, mm3)
        schur = schur - term(1, dx_ref[r], lower, False, mm3)
        schur = schur - term(2, yu_ref[r], up_ref[r, 1], True, mm1)
        schur = schur - term(3, yl_ref[r], cy_ref[r], False, mm1)
        schur = schur - term(4, zu_ref[r], up_ref[r, 2], True, mm1)
        schur = schur - term(5, zl_ref[r], cz_ref[r], False, mm1)
        work[r] = schur
        return carry

    lax.fori_loop(0, count, gather, 0, unroll=2)
    ul_factors(work)

    own = split(prod_ref[...])
    around = [split(near_ref[k]) for k in range(6)]

    def finish(r, carry):
        y = work[r]
        low = y.astype(BF16)
        factor_ref[r, 0] = low
        total = mm1(own, low, 1, 1)
        for k in range(6):
            block = (-(mm3 if k < 2 else mm1)(y, solved[r, k], 1, 1)).astype(BF16)
            factor_ref[r, 1 + k] = block
            total = total + mm1(around[k], block, 1, 1)
        total = total[:count] + total[count : 2 * count] + total[2 * count :]
        keep = lax.broadcasted_iota(jnp.int32, total.shape, 0) == r
        applied_ref[...] = jnp.where(keep, total, applied_ref[...])
        return carry

    applied_ref[...] = jnp.zeros_like(applied_ref)
    lax.fori_loop(0, count, finish, 0, unroll=2)


VM = pl.BlockSpec(memory_space=pltpu.VMEM)
SM = pl.BlockSpec(memory_space=pltpu.SMEM)


def local(diag_blocks, up_blocks, pattern, vector_in):
    rows, width = diag_blocks.shape[0], diag_blocks.shape[1]
    block = jax.ShapeDtypeStruct((rows, width, width), BF16)
    vec = pltpu.VMEM((3, rows, width), F32)
    stack = pltpu.VMEM((rows, width, width), BF16)
    prod, near, dx, edge, cy, cz, yu, yl, zu, zl = pl.pallas_call(
        functools.partial(exchange_kernel, lax.axis_size("help"), lax.axis_size("dom")),
        out_shape=(
            jax.ShapeDtypeStruct((rows, width), F32),
            jax.ShapeDtypeStruct((6, rows, width), F32),
            jax.ShapeDtypeStruct((rows + 2, width, width), F32),
            jax.ShapeDtypeStruct((1, width, width), F32),
        )
        + (block,) * 6,
        in_specs=[VM] * 3,
        out_specs=(VM,) * 10,
        scratch_shapes=[pltpu.VMEM((rows, width, width), F32)]
        + [stack] * 3
        + [vec] * 5
        + [pltpu.SemaphoreType.DMA((MESSAGES,)), pltpu.SemaphoreType.DMA((MESSAGES,))],
        name="exchange",
        compiler_params=pltpu.CompilerParams(
            collective_id=0, has_side_effects=True, vmem_limit_bytes=40 << 20
        ),
    )(diag_blocks, up_blocks, vector_in)
    factor, applied = pl.pallas_call(
        rows_kernel,
        out_shape=(
            jax.ShapeDtypeStruct((rows, 7, width, width), BF16),
            jax.ShapeDtypeStruct((rows, width), F32),
        ),
        in_specs=[SM] + [VM] * 12,
        out_specs=(VM, VM),
        scratch_shapes=[
            pltpu.VMEM((rows, width, width), F32),
            pltpu.VMEM((rows, 6, width, width), F32),
        ],
        name="rows",
        compiler_params=pltpu.CompilerParams(vmem_limit_bytes=40 << 20),
    )(pattern, diag_blocks, up_blocks, edge, dx, cy, cz, yu, yl, zu, zl, prod, near)
    return (factor, applied)


def solution(mesh):
    in_specs = (
        P(("dom", "help"), None, None),
        P(("dom", "help"), None, None, None),
        P(("dom", "help"), None),
        P(("dom", "help"), None),
    )
    out_specs = (P(("dom", "help"), None, None, None), P(("dom", "help"), None))
    return jax.shard_map(local, mesh=mesh, in_specs=in_specs, out_specs=out_specs, check_vma=False)
```

```python
import functools

import jax
import jax.numpy as jnp
from jax import lax
from jax.experimental import pallas as pl
from jax.experimental.pallas import tpu as pltpu
from jax.sharding import PartitionSpec as P

PLANE = 4
SUB = 32
CHUNKS = 4
MESSAGES = 17 + 4 * CHUNKS
HIGH = lax.Precision.HIGHEST
F32 = jnp.float32
BF16 = jnp.bfloat16


def mm(a, b, ca, cb):
    return lax.dot_general(
        a, b, (((ca,), (cb,)), ((), ())), precision=HIGH, preferred_element_type=F32
    )


def mm1(a, b, ca, cb):
    return lax.dot_general(
        a.astype(BF16), b.astype(BF16), (((ca,), (cb,)), ((), ())), preferred_element_type=F32
    )


def halves(a):
    high = a.astype(BF16)
    return high, (a - high.astype(F32)).astype(BF16)


def mm3(a, b, ca, cb):
    (ah, al), (bh, bl) = halves(a), halves(b)
    return mm1(ah, bh, ca, cb) + (mm1(ah, bl, ca, cb) + mm1(al, bh, ca, cb))


def split(v):
    high = v.astype(BF16).astype(F32)
    rest = v - high
    mid = rest.astype(BF16).astype(F32)
    return jnp.concatenate([high, mid, rest - mid], 0).astype(BF16)


def mv(parts, matrix, cb):
    high, low = halves(matrix)
    total = mm1(parts, high, 1, cb) + mm1(parts, low, 1, cb)
    n = total.shape[0] // 3
    return total[:n] + (total[n : 2 * n] + total[2 * n :])


def small_factors(groups):
    lane = lax.broadcasted_iota(jnp.int32, (8, 128), 1)
    sub = lax.broadcasted_iota(jnp.int32, (8, 128), 0)
    within = lane % SUB
    base = lane - within
    for top in range(SUB // 8 - 1, -1, -1):
        ahead = [
            [
                [jnp.take_along_axis(tiles[t], base + 8 * top + i, axis=1) for t in range(top + 1)]
                for i in range(8)
            ]
            for tiles in groups
        ]
        for at in range(7, -1, -1):
            j = 8 * top + at
            here = within == j
            for tiles, cols in zip(groups, ahead):
                scale = lax.rsqrt(cols[at][top][at : at + 1, :])
                scaled = [cols[at][t] * scale for t in range(top + 1)]
                for i in range(at - 1, -1, -1):
                    weight = cols[i][top][at : at + 1, :] * scale
                    cols[i] = [cols[i][t] - scaled[t] * weight for t in range(top + 1)]
                row = jnp.where(here[:1], 1.0, tiles[top][at : at + 1, :]) * scale
                final = jnp.where(within[:1] >= j, row, 0.0)
                for t in range(top + 1):
                    new = jnp.where(here, 0.0, tiles[t]) - scaled[t] * row
                    if t == top:
                        new = jnp.where(sub < at, new, jnp.where(sub == at, final, tiles[t]))
                    tiles[t] = new
    return groups


def ul_factors(work, between=None):
    count, width = work.shape[0], work.shape[1]
    pack = width // SUB
    lane = lax.broadcasted_iota(jnp.int32, (SUB, width), 1)
    sub = lax.broadcasted_iota(jnp.int32, (SUB, width), 0)
    owner = lane // SUB
    for j in range(pack - 1, -1, -1):
        lo = SUB * j
        packed = []
        panels = []
        for g in range(count // pack):
            block = jnp.zeros((SUB, width), F32)
            panel = []
            for b in range(pack):
                rows = work[g * pack + b, lo : lo + SUB, :]
                shift = (SUB * (b - j)) % width
                moved = pltpu.roll(rows, shift, 1) if shift else rows
                block = jnp.where(owner == b, moved, block)
                panel.append(jnp.where(owner == j, (lane - lo == sub).astype(F32), rows))
            packed.append([block[8 * t : 8 * t + 8] for t in range(SUB // 8)])
            panels.append(jnp.concatenate(panel, 0))
        small_factors(packed)
        for g in range(count // pack):
            small = jnp.concatenate(packed[g], 0)
            spread = jnp.concatenate(
                [jnp.where(owner == b, small, 0.0) for b in range(pack)], 0
            )
            scaled = mm3(spread, panels[g], 1, 0)
            for b in range(pack):
                at = g * pack + b
                v = scaled[SUB * b : SUB * b + SUB]
                work[at, lo : lo + SUB, :] = jnp.where(lane >= lo, v, 0.0)
                if lo:
                    change = mm3(v, v, 0, 0)
                    full = lax.broadcasted_iota(jnp.int32, (lo, width), 1) // SUB
                    work[at, :lo, :] = jnp.where(full == j, 0.0, work[at, :lo, :]) - change[:lo]
        if between:
            between(j)


def exchange_kernel(
    line_count, dom_count, diag_ref, up_ref, x_ref, prod_ref, near_ref, dx_ref, edge_ref, cy_ref,
    cz_ref, yu_ref, yl_ref, zu_ref, zl_ref, work, cy_own, cz_own, low, upt, from_up, from_low,
    prod_up, prod_low, send_sem, recv_sem
):
    rows = x_ref.shape[0]
    dom = lax.axis_index("dom")
    line = lax.axis_index("help")
    spot = lax.rem(dom, PLANE)
    exists = (
        (line < line_count - 1, line > 0),
        (spot < PLANE - 1, spot > 0),
        (dom + PLANE < dom_count, dom >= PLANE),
    )
    target = (
        ((dom, line + 1), (dom, line - 1)),
        ((dom + 1, line), (dom - 1, line)),
        ((dom + PLANE, line), (dom - PLANE, line)),
    )
    barrier = pltpu.get_barrier_semaphore()
    partners = jnp.int32(0)
    for d in range(3):
        for s in range(2):
            partners = partners + exists[d][s].astype(jnp.int32)

            @pl.when(exists[d][s])
            def _(d=d, s=s):
                pl.semaphore_signal(
                    barrier, inc=1, device_id=target[d][s], device_id_type=pl.DeviceIdType.MESH
                )

    pl.semaphore_wait(barrier, partners)
    messages = []

    def send(d, s, src, dst):
        m = len(messages)
        copy = pltpu.make_async_remote_copy(
            src_ref=src,
            dst_ref=dst,
            send_sem=send_sem.at[m],
            recv_sem=recv_sem.at[m],
            device_id=target[d][s],
            device_id_type=pl.DeviceIdType.MESH,
        )
        messages.append((d, s, copy))

        @pl.when(exists[d][s])
        def _():
            copy.start()

        return m

    def received(ids):
        for m in ids:
            d, s, copy = messages[m]

            @pl.when(exists[d][1 - s])
            def _(copy=copy):
                copy.wait_recv()

    def blank(d, s, ref):
        @pl.when(jnp.logical_not(exists[d][s]))
        def _():
            ref[...] = jnp.zeros_like(ref)

    blank(0, 1, edge_ref)
    blank(1, 1, cy_ref)
    blank(2, 1, cz_ref)
    blank(0, 1, dx_ref.at[0])
    blank(0, 0, dx_ref.at[rows + 1])
    blank(1, 0, yu_ref)
    blank(1, 1, yl_ref)
    blank(2, 0, zu_ref)
    blank(2, 1, zl_ref)
    for d in range(3):
        blank(d, 0, from_up.at[d])
        blank(d, 1, from_low.at[d])
        blank(d, 0, prod_up.at[d])
        blank(d, 1, prod_low.at[d])
    first = [send(d, 1, x_ref, from_up.at[d]) for d in range(3)]
    late = [send(0, 0, up_ref.at[rows - 1, 0], edge_ref.at[0])]
    cy_own[...] = up_ref[:, 1].astype(BF16)
    cz_own[...] = up_ref[:, 2].astype(BF16)
    vec = x_ref[...]
    parts = split(vec)
    at_row = lax.broadcasted_iota(jnp.int32, vec.shape, 0)
    for d in range(3):
        total = jnp.zeros_like(vec)
        for r in range(rows):
            total = jnp.where(at_row == r, mv(parts, up_ref[r, d], 0), total)
        upt[d] = total
    for d in range(3):
        first.append(send(d, 0, upt.at[d], from_low.at[d]))
    late.append(send(1, 0, cy_own, cy_ref))
    late.append(send(2, 0, cz_own, cz_ref))
    work[...] = diag_ref[...]

    def above(own, edge):
        return jnp.where(at_row == rows - 1, edge[:1], pltpu.roll(own, rows - 1, 0))

    def below(own, edge):
        return jnp.where(at_row == 0, edge[rows - 1 : rows], pltpu.roll(own, 1, 0))

    def between(j):
        if j == work.shape[1] // SUB - 1:
            received(first)
            total = below(upt[0], from_low[0]) + from_low[1] + from_low[2]
            ups = [split(v) for v in (above(vec, from_up[0]), from_up[1], from_up[2])]
            for r in range(rows):
                part = mv(parts, diag_ref[r], 1)
                for d in range(3):
                    part = part + mv(ups[d], up_ref[r, d], 1)
                total = total + jnp.where(at_row == r, part, 0.0)
            prod_ref[...] = total
        if j == work.shape[1] // SUB - 2:
            for d in range(3):
                late.append(send(d, 1, prod_ref, prod_up.at[d]))
                late.append(send(d, 0, prod_ref, prod_low.at[d]))

    ul_factors(work, between)
    half = rows // CHUNKS
    for h in range(CHUNKS):
        for r in range(half * h, half * h + half):
            y = work[r]
            inv = mm3(y, y, 0, 0)
            dx_ref[r + 1] = inv
            low[r] = inv.astype(BF16)
        part = pl.ds(half * h, half)
        late.append(send(2, 0, low.at[part], zl_ref.at[part]))
        late.append(send(2, 1, low.at[part], zu_ref.at[part]))
        late.append(send(1, 0, low.at[part], yl_ref.at[part]))
        late.append(send(1, 1, low.at[part], yu_ref.at[part]))
        if h == CHUNKS - 1:
            late.append(send(0, 0, dx_ref.at[rows], dx_ref.at[0]))
        if h == 0:
            late.append(send(0, 1, dx_ref.at[1], dx_ref.at[rows + 1]))
    received(late)
    total = prod_ref[...]
    near_ref[0] = above(total, prod_up[0])
    near_ref[1] = below(total, prod_low[0])
    near_ref[2] = prod_up[1]
    near_ref[3] = prod_low[1]
    near_ref[4] = prod_up[2]
    near_ref[5] = prod_low[2]
    for d, s, copy in messages:

        @pl.when(exists[d][s])
        def _(copy=copy):
            copy.wait_send()


def rows_kernel(
    pattern_ref, diag_ref, up_ref, edge_ref, dx_ref, cy_ref, cz_ref, yu_ref, yl_ref, zu_ref,
    zl_ref, prod_ref, near_ref, factor_ref, applied_ref, work, solved
):
    count = work.shape[0]

    def gather(r, carry):
        schur = diag_ref[r]

        def term(k, inv, coupling, plus, mul):
            w = pattern_ref[r, k].astype(F32) * mul(inv, coupling, 1, 1 if plus else 0)
            solved[r, k] = w
            return mul(coupling, w, 1 if plus else 0, 0)

        lower = jnp.where(r == 0, edge_ref[0], up_ref[jnp.maximum(r - 1, 0), 0])
        schur = schur - term(0, dx_ref[r + 2], up_ref[r, 0], True, mm3)
        schur = schur - term(1, dx_ref[r], lower, False, mm3)
        schur = schur - term(2, yu_ref[r], up_ref[r, 1], True, mm1)
        schur = schur - term(3, yl_ref[r], cy_ref[r], False, mm1)
        schur = schur - term(4, zu_ref[r], up_ref[r, 2], True, mm1)
        schur = schur - term(5, zl_ref[r], cz_ref[r], False, mm1)
        work[r] = schur
        return carry

    lax.fori_loop(0, count, gather, 0, unroll=4)
    ul_factors(work)

    own = split(prod_ref[...])
    around = [split(near_ref[k]) for k in range(6)]

    def finish(r, carry):
        y = work[r]
        low = y.astype(BF16)
        factor_ref[r, 0] = low
        total = mm1(own, low, 1, 1)
        for k in range(6):
            block = (-(mm3 if k < 2 else mm1)(y, solved[r, k], 1, 1)).astype(BF16)
            factor_ref[r, 1 + k] = block
            total = total + mm1(around[k], block, 1, 1)
        total = total[:count] + total[count : 2 * count] + total[2 * count :]
        keep = lax.broadcasted_iota(jnp.int32, total.shape, 0) == r
        applied_ref[...] = jnp.where(keep, total, applied_ref[...])
        return carry

    applied_ref[...] = jnp.zeros_like(applied_ref)
    lax.fori_loop(0, count, finish, 0, unroll=4)


VM = pl.BlockSpec(memory_space=pltpu.VMEM)
SM = pl.BlockSpec(memory_space=pltpu.SMEM)


def local(diag_blocks, up_blocks, pattern, vector_in):
    rows, width = diag_blocks.shape[0], diag_blocks.shape[1]
    block = jax.ShapeDtypeStruct((rows, width, width), BF16)
    vec = pltpu.VMEM((3, rows, width), F32)
    stack = pltpu.VMEM((rows, width, width), BF16)
    prod, near, dx, edge, cy, cz, yu, yl, zu, zl = pl.pallas_call(
        functools.partial(exchange_kernel, lax.axis_size("help"), lax.axis_size("dom")),
        out_shape=(
            jax.ShapeDtypeStruct((rows, width), F32),
            jax.ShapeDtypeStruct((6, rows, width), F32),
            jax.ShapeDtypeStruct((rows + 2, width, width), F32),
            jax.ShapeDtypeStruct((1, width, width), F32),
        )
        + (block,) * 6,
        in_specs=[VM] * 3,
        out_specs=(VM,) * 10,
        scratch_shapes=[pltpu.VMEM((rows, width, width), F32)]
        + [stack] * 3
        + [vec] * 5
        + [pltpu.SemaphoreType.DMA((MESSAGES,)), pltpu.SemaphoreType.DMA((MESSAGES,))],
        name="exchange",
        compiler_params=pltpu.CompilerParams(
            collective_id=0, has_side_effects=True, vmem_limit_bytes=40 << 20
        ),
    )(diag_blocks, up_blocks, vector_in)
    factor, applied = pl.pallas_call(
        rows_kernel,
        out_shape=(
            jax.ShapeDtypeStruct((rows, 7, width, width), BF16),
            jax.ShapeDtypeStruct((rows, width), F32),
        ),
        in_specs=[SM] + [VM] * 12,
        out_specs=(VM, VM),
        scratch_shapes=[
            pltpu.VMEM((rows, width, width), F32),
            pltpu.VMEM((rows, 6, width, width), F32),
        ],
        name="rows",
        compiler_params=pltpu.CompilerParams(vmem_limit_bytes=40 << 20),
    )(pattern, diag_blocks, up_blocks, edge, dx, cy, cz, yu, yl, zu, zl, prod, near)
    return (factor, applied)


def solution(mesh):
    in_specs = (
        P(("dom", "help"), None, None),
        P(("dom", "help"), None, None, None),
        P(("dom", "help"), None),
        P(("dom", "help"), None),
    )
    out_specs = (P(("dom", "help"), None, None, None), P(("dom", "help"), None))
    return jax.shard_map(local, mesh=mesh, in_specs=in_specs, out_specs=out_specs, check_vma=False)
```
